32 devices in a mesh: cuts: 2 (over x), region: 16 (over z, y, core).
Axes of the slice: x: 2, y: 2, z: 4, core: 2. Of those that a mesh axis runs over, the one named last changes fastest.
Arguments:
- objects: float32 [2, 2, 4096, 1024], P('cuts', None, 'region'), may hold values from -4 to 4
- probes: bfloat16 [4, 2, 256, 256], replicated, may hold values from -4 to 4
- amplitudes: float32 [64, 256, 256], P('region'), may hold values from 0.2 to 2.5
- prop_phase: float32 [256, 256], replicated, may hold values from -3.140625 to 3.140625
- scan_rows: int32 [64], P('region'), may hold values from -128 to 128, as said below
- scan_cols: int32 [64], P('region'), may hold values from 0 to 768
- probe_choice: int32 [64], P('region'), may hold values from 0 to 3
Outputs:
- gradient: float32 [2, 2, 4096, 1024], P('cuts', None, 'region')
The draws below stay inside these ranges and needn't reach their ends.
Inputs may be any that keep to these rules, and one draw needn't show every extreme that they name: `scan_rows`: in every region, half of the positions start between 64 and 128 rows above the band's first row, and the other half end between 64 and 128 rows below its last row.
All inputs are finite; a program needn't handle non-finite values.
Results may differ from the reference program's by a relative error of at most 0.039.
Values may be sent and summed in bfloat16 or wider, within the bound.
A program may use at most 64 MiB of HBM per device.

```python
import math
import jax
import jax.numpy as jnp
from jax import lax

PATCH = 256
HALO = 128
SLICES = 2
BATCHES = 4
PER_BATCH = 1
PROBES = 4
ROWS = 256
COLS = 1024
POS_DEV = 4
NPOS = 64
NROWS = 4096


def draw_scan_rows(key, part):
    key_order = jax.random.fold_in(key, 11)
    key_upper = jax.random.fold_in(key, 12)
    key_lower = jax.random.fold_in(key, 13)
    regions = NPOS // POS_DEV
    upper_rows = jax.random.randint(key_upper, (regions, POS_DEV), -HALO, -(HALO // 2) + 1, dtype=jnp.int32)
    lower_rows = jax.random.randint(key_lower, (regions, POS_DEV), ROWS - PATCH + HALO // 2, ROWS - PATCH + HALO + 1, dtype=jnp.int32)
    scores = jax.random.randint(key_order, (regions, POS_DEV), 0, 1 << 20, dtype=jnp.int32) * POS_DEV + jnp.arange(POS_DEV, dtype=jnp.int32)[None, :]
    ranking = jnp.argsort(jnp.argsort(scores, axis=1), axis=1)
    return jnp.where(ranking < POS_DEV // 2, upper_rows, lower_rows).astype(jnp.int32).reshape(-1)


def touch_ends(values, key, least, largest):
    dims = values.shape
    index_at = [jax.random.randint(jax.random.fold_in(key, axis), (), 0, dims[axis]) for axis in range(len(dims))]
    values = values.at[tuple(index_at)].set(least)
    longest = dims.index(max(dims))
    index_at[longest] = (index_at[longest] + 1) % dims[longest]
    return values.at[tuple(index_at)].set(largest)


def steps_of(rng, dims, cuts, least, top_value):
    def one(dim, shards_of):
        draws = jax.random.uniform(jax.random.fold_in(jax.random.fold_in(rng, 6), dim), (shards_of,), jnp.float32, least / len(cuts), top_value / len(cuts))
        return jnp.repeat(jnp.exp(draws), dims[dim] // shards_of).reshape((-1,) + (1,) * (len(dims) - dim - 1))

    level = one(*cuts[0])
    for cut in cuts[1:]:
        level = level * one(*cut)
    return level


def gaussian(own_key, shape, width, most, split=(), held_as=jnp.bfloat16):
    drawn = jax.random.normal(own_key, shape, jnp.float32) * width
    if len(split) > 0:
        drawn = steps_of(own_key, shape, split, -0.22, 0.18) * drawn
    return jnp.clip(drawn, min=-most, max=most).astype(held_as)


def setup_inputs(seed: int = 0) -> dict:
    key_list = jax.random.split(jax.random.key(seed), 8)
    objects = gaussian(key_list[0], (SLICES, 2, NROWS, COLS), 0.7, 4.0, ((0, 2), (2, 16)), jnp.float32)
    probes = gaussian(key_list[1], (PROBES, 2, PATCH, PATCH), 0.7, 4.0)
    amplitudes = jnp.clip(jnp.exp(math.log(2.5) - 2.5257286 * jax.random.uniform(key_list[2], (NPOS, PATCH, PATCH), jnp.float32) ** steps_of(key_list[2], (NPOS, PATCH, PATCH), ((0, 16),), -0.2, 0.2)), 0.2, 2.5)
    prop_phase = jnp.clip(jax.random.uniform(key_list[3], (PATCH, PATCH), jnp.float32, -3.140625, 3.140625), -3.140625, 3.140625)
    scan_rows = draw_scan_rows(jax.random.fold_in(key_list[7], 71), 0)
    scan_cols = touch_ends(jax.random.randint(key_list[5], (NPOS,), 0, COLS - PATCH + 1), jax.random.fold_in(key_list[5], 1), 0, COLS - PATCH).astype(jnp.int32)
    probe_choice = touch_ends(jax.random.randint(key_list[6], (NPOS,), 0, PROBES), jax.random.fold_in(key_list[6], 1), 0, PROBES - 1).astype(jnp.int32)
    return {"objects": objects, "probes": probes, "amplitudes": amplitudes, "prop_phase": prop_phase, "scan_rows": scan_rows, "scan_cols": scan_cols, "probe_choice": probe_choice}


modulus_floor = 0.25

def widened(narrow):
    return lax.optimization_barrier(narrow).astype(jnp.float32)

def dft_tables(length, direction):
    indices = jnp.arange(length, dtype=jnp.int32)
    product = indices[:, None] * indices[None, :] % length
    angles = product.astype(jnp.float32) * (2.0 * jnp.pi / length)
    scaling = 1.0 / jnp.sqrt(jnp.float32(length))
    return jnp.stack([jnp.cos(angles) * scaling, direction * jnp.sin(angles) * scaling]).astype(jnp.bfloat16)

def complex_join(part_stack):
    return jnp.stack([part_stack[0, :, 0] - part_stack[1, :, 1], part_stack[0, :, 1] + part_stack[1, :, 0]], axis=1)

def transform(input_field, dft_table):
    wide_table = dft_table.astype(jnp.float32)
    narrow_field = widened(input_field.astype(jnp.bfloat16))
    left_part = jnp.einsum('ajk,nckl->ancjl', wide_table, narrow_field)
    middle = widened(complex_join(left_part).astype(jnp.bfloat16))
    right_part = jnp.einsum('nckl,alm->anckm', middle, wide_table)
    return complex_join(right_part)

def multiply_complex(left_field, right_field):
    real_part = left_field[..., 0, :, :] * right_field[..., 0, :, :] - left_field[..., 1, :, :] * right_field[..., 1, :, :]
    imag_part = left_field[..., 0, :, :] * right_field[..., 1, :, :] + left_field[..., 1, :, :] * right_field[..., 0, :, :]
    return jnp.stack([real_part, imag_part], axis=-3)

def multiply_conjugate(left_field, right_field):
    real_part = left_field[..., 0, :, :] * right_field[..., 0, :, :] + left_field[..., 1, :, :] * right_field[..., 1, :, :]
    imag_part = left_field[..., 0, :, :] * right_field[..., 1, :, :] - left_field[..., 1, :, :] * right_field[..., 0, :, :]
    return jnp.stack([real_part, imag_part], axis=-3)

def propagate(input_field, optics):
    propagator, forward_table, inverse_table = optics
    return transform(multiply_complex(propagator, transform(input_field, forward_table)), inverse_table)

def propagate_adjoint(input_field, optics):
    propagator, forward_table, inverse_table = optics
    return transform(multiply_conjugate(propagator, transform(input_field, forward_table)), inverse_table)

def reference(objects, probes, amplitudes, prop_phase, scan_rows, scan_cols, probe_choice):
    slice_count = objects.shape[0]
    total_rows = objects.shape[2]
    rim_depth = PATCH // 2
    per_region = BATCHES * PER_BATCH
    optics = (jnp.stack([jnp.cos(prop_phase), jnp.sin(prop_phase)]), dft_tables(PATCH, -1.0), dft_tables(PATCH, 1.0))
    zero_index = jnp.zeros((), jnp.int32)
    window_steps = jnp.arange(PATCH, dtype=jnp.int32)

    def visit_position(running, position):
        region = position // per_region
        top_row = (region * ROWS + scan_rows[position]).astype(jnp.int32)
        left_col = scan_cols[position].astype(jnp.int32)
        row_ids = ((top_row + total_rows + window_steps) % total_rows).astype(jnp.int32)
        band_part = jnp.take(objects, row_ids, axis=2)
        window = lax.dynamic_slice(band_part, (zero_index, zero_index, zero_index, left_col), (slice_count, 2, PATCH, PATCH))
        current = probes[probe_choice[position]][None]
        measured = amplitudes[position][None]
        stored = []
        for slice_index in range(slice_count):
            stored.append(current)
            exit_field = multiply_complex(widened(current), window[slice_index][None])
            if slice_index < slice_count - 1:
                current = propagate(exit_field, optics).astype(jnp.bfloat16)
            else:
                far_field = transform(exit_field, optics[1])
                modulus = jnp.sqrt(far_field[:, 0] * far_field[:, 0] + far_field[:, 1] * far_field[:, 1])
                factor = 1.0 - measured / jnp.maximum(modulus, modulus_floor)
                current = transform(far_field * factor[:, None], optics[2]).astype(jnp.bfloat16)
        pieces = [None] * slice_count
        for slice_index in reversed(range(slice_count)):
            arriving = widened(current)
            pieces[slice_index] = multiply_conjugate(widened(stored[slice_index]), arriving)[0]
            if slice_index > 0:
                backward = multiply_conjugate(window[slice_index][None], arriving)
                current = propagate_adjoint(backward, optics).astype(jnp.bfloat16)
        deposit_block = jnp.stack(pieces)
        corner = (zero_index, zero_index, (top_row + rim_depth).astype(jnp.int32), left_col)
        existing = lax.dynamic_slice(running, corner, deposit_block.shape)
        return (lax.dynamic_update_slice(running, existing + deposit_block, corner), None)
    padded_shape = (slice_count, 2, total_rows + 2 * rim_depth, objects.shape[3])
    summed, unused = lax.scan(visit_position, jnp.zeros(padded_shape, jnp.float32), jnp.arange(NPOS, dtype=jnp.int32))
    gradient = summed[:, :, rim_depth:rim_depth + total_rows]
    gradient = gradient.at[:, :, :rim_depth].add(summed[:, :, total_rows + rim_depth:])
    gradient = gradient.at[:, :, total_rows - rim_depth:].add(summed[:, :, :rim_depth])
    return gradient
```

```python
import functools
import jax
import jax.numpy as jnp
import numpy as np
from jax import lax
from jax.experimental import pallas as pl
from jax.experimental.pallas import tpu as pltpu
from jax.sharding import PartitionSpec as P

modulus_floor = 0.25
LANES = 128
SUBLANES = 8
VMEM = pl.BlockSpec(memory_space=pltpu.VMEM)
SMEM = pl.BlockSpec(memory_space=pltpu.SMEM)
LIMIT = pltpu.CompilerParams(vmem_limit_bytes=60000 * 1024)


def dft_blocks(side):
    indices = np.arange(side)
    angles = (indices[:, None] * indices[None, :] % side) * (2.0 * np.pi / side)
    real = np.cos(angles) / np.sqrt(side)
    imag = np.sin(angles) / np.sqrt(side)
    tables = []
    for sign in (-1.0, 1.0):
        tables.append(np.block([[real, -sign * imag], [sign * imag, real]]))
        tables.append(np.block([[real, sign * imag], [-sign * imag, real]]))
    return jnp.asarray(np.stack(tables), dtype=jnp.bfloat16)


def split_col(col, cols, side):
    base = jnp.minimum(col // LANES, (cols - side) // LANES - 1) * LANES
    return pl.multiple_of(base, LANES), col - base


def cut_window(ext, plane, row, col, side):
    base, shift = split_col(col, ext.shape[2], side)
    top = pl.multiple_of(row // SUBLANES * SUBLANES, SUBLANES)
    tall = side + SUBLANES
    block = ext[plane, pl.ds(top, tall), pl.ds(base, side + LANES)]
    block = pltpu.roll(block, lax.rem(tall + top - row, tall), axis=0)[:side]
    back = lax.rem(LANES - shift + LANES, LANES)
    chunks = [
        pltpu.roll(block[:, j : j + LANES], back, axis=1) for j in range(0, side + LANES, LANES)
    ]
    lane = lax.broadcasted_iota(jnp.int32, (side, LANES), 1)
    keep = lane < LANES - shift
    return jnp.concatenate(
        [jnp.where(keep, chunks[j], chunks[j + 1]) for j in range(len(chunks) - 1)], axis=1
    )


def add_window(grad, plane, row, col, field):
    side = field.shape[0]
    base, shift = split_col(col, grad.shape[2], side)
    top = pl.multiple_of(row // SUBLANES * SUBLANES, SUBLANES)
    tall = side + SUBLANES
    field = jnp.concatenate([field, jnp.zeros((SUBLANES, side), field.dtype)], axis=0)
    field = pltpu.roll(field, row - top, axis=0)
    ahead = lax.rem(shift, LANES)
    chunks = [pltpu.roll(field[:, j : j + LANES], ahead, axis=1) for j in range(0, side, LANES)]
    lane = lax.broadcasted_iota(jnp.int32, (tall, LANES), 1)
    keep = lane >= shift
    zero = jnp.zeros((tall, LANES), field.dtype)
    parts = [zero] + chunks + [zero]
    placed = jnp.concatenate(
        [jnp.where(keep, parts[j + 1], parts[j]) for j in range(len(chunks) + 1)], axis=1
    )
    where = (plane, pl.ds(top, tall), pl.ds(base, side + LANES))
    grad[where] = grad[where] + placed


def cut_kernel(side, half, rows, cols, cut, band, low, high, own, sent, ext):
    rim = low.shape[1]
    band_rows = band.shape[1]
    ext[:, :rim] = low[...].astype(jnp.float32)
    ext[:, rim : rim + band_rows] = band[...]
    ext[:, rim + band_rows : 2 * rim + band_rows] = high[...].astype(jnp.float32)
    for index in range(half):
        for target, first in ((own, cut[0] * half), (sent, (1 - cut[0]) * half)):
            position = first + index
            for plane in range(2):
                target[index, plane] = cut_window(
                    ext, plane, rows[position] + rim, cols[position], side
                ).astype(target.dtype)


def dot(left, right):
    return jnp.dot(left, right, preferred_element_type=jnp.float32)


def transform(field, tables, which):
    side = field[0].shape[0]
    stacked = jnp.concatenate([field[0].astype(jnp.bfloat16), field[1].astype(jnp.bfloat16)], axis=0)
    middle = dot(tables[which], stacked).astype(jnp.bfloat16)
    beside = jnp.concatenate([middle[:side], middle[side:]], axis=1)
    result = dot(beside, tables[which + 1])
    return result[:, :side], result[:, side:]


def multiply(left, right):
    return left[0] * right[0] - left[1] * right[1], left[0] * right[1] + left[1] * right[0]


def multiply_conjugate(left, right):
    return left[0] * right[0] + left[1] * right[1], left[0] * right[1] - left[1] * right[0]


def narrowed(field):
    return tuple(part.astype(jnp.bfloat16).astype(jnp.float32) for part in field)


def one_position(psi0, object0, object1, measured, wave, tables):
    psi1 = narrowed(
        transform(multiply(wave, transform(multiply(psi0, object0), tables, 0)), tables, 2)
    )
    far = transform(multiply(psi1, object1), tables, 0)
    modulus = jnp.sqrt(far[0] * far[0] + far[1] * far[1])
    factor = 1.0 - measured / jnp.maximum(modulus, modulus_floor)
    g1 = narrowed(transform((far[0] * factor, far[1] * factor), tables, 2))
    d1 = multiply_conjugate(psi1, g1)
    back = transform(multiply_conjugate(object1, g1), tables, 0)
    g0 = narrowed(transform(multiply_conjugate(wave, back), tables, 2))
    return multiply_conjugate(psi0, g0), d1


def wide(ref, *index):
    return ref[index + (0,)].astype(jnp.float32), ref[index + (1,)].astype(jnp.float32)


def wave_kernel(half, choice, cut, own, other, probes, amps, wave, tables, mine, theirs):
    c = cut[0]
    first = c == 0
    for index in range(half):
        position = c * half + index
        psi0 = wide(probes, choice[position])
        a = wide(own, index)
        b = wide(other, index)
        object0 = tuple(jnp.where(first, x, y) for x, y in zip(a, b))
        object1 = tuple(jnp.where(first, y, x) for x, y in zip(a, b))
        d0, d1 = one_position(psi0, object0, object1, amps[position], (wave[0], wave[1]), tables)
        for plane in range(2):
            mine[index, plane] = jnp.where(first, d0[plane], d1[plane]).astype(mine.dtype)
            theirs[index, plane] = jnp.where(first, d1[plane], d0[plane]).astype(theirs.dtype)


def deposit_kernel(half, rows, cols, cut, mine, arrived, inner, low, high, grad):
    rim = low.shape[1]
    band_rows = inner.shape[1]
    grad[...] = jnp.zeros_like(grad)
    for index in range(half):
        for source, first in ((mine, cut[0] * half), (arrived, (1 - cut[0]) * half)):
            position = first + index
            for plane in range(2):
                add_window(
                    grad, plane, rows[position] + rim, cols[position],
                    source[index, plane].astype(jnp.float32),
                )
    low[...] = grad[:, :rim].astype(low.dtype)
    inner[...] = grad[:, rim : rim + band_rows]
    high[...] = grad[:, rim + band_rows : 2 * rim + band_rows].astype(high.dtype)


def shards(objects, probes, amplitudes, prop_phase, scan_rows, scan_cols, probe_choice):
    side = probes.shape[-1]
    rim = side // 2
    count = lax.axis_size("region")
    band = objects[0]
    band_rows, columns = band.shape[1:]
    half = scan_rows.shape[0] // 2
    cut = lax.axis_index("cuts").astype(jnp.int32)[None]
    forward = [(i, (i + 1) % count) for i in range(count)]
    backward = [(i, (i - 1) % count) for i in range(count)]
    swap = [(0, 1), (1, 0)]
    low = lax.ppermute(band[:, band_rows - rim :].astype(jnp.bfloat16), "region", forward)
    high = lax.ppermute(band[:, :rim].astype(jnp.bfloat16), "region", backward)
    wave = jnp.stack([jnp.cos(prop_phase), jnp.sin(prop_phase)])
    tables = dft_blocks(side)
    fields = jax.ShapeDtypeStruct((half, 2, side, side), jnp.bfloat16)
    tall = pltpu.VMEM((2, band_rows + 2 * rim + SUBLANES, columns), jnp.float32)
    own, sent = pl.pallas_call(
        functools.partial(cut_kernel, side, half),
        out_shape=(fields, fields),
        in_specs=[SMEM] * 3 + [VMEM] * 3,
        out_specs=(VMEM, VMEM),
        scratch_shapes=[tall],
        compiler_params=LIMIT,
    )(scan_rows, scan_cols, cut, band, low, high)
    other = lax.ppermute(sent, "cuts", swap)
    mine, theirs = pl.pallas_call(
        functools.partial(wave_kernel, half),
        out_shape=(fields, fields),
        in_specs=[SMEM] * 2 + [VMEM] * 6,
        out_specs=(VMEM, VMEM),
        compiler_params=LIMIT,
    )(probe_choice, cut, own, other, probes, amplitudes, wave, tables)
    arrived = lax.ppermute(theirs, "cuts", swap)
    edge = jax.ShapeDtypeStruct((2, rim, columns), jnp.bfloat16)
    inner, up, down = pl.pallas_call(
        functools.partial(deposit_kernel, half),
        out_shape=(jax.ShapeDtypeStruct(band.shape, jnp.float32), edge, edge),
        in_specs=[SMEM] * 3 + [VMEM] * 2,
        out_specs=(VMEM, VMEM, VMEM),
        scratch_shapes=[tall],
        compiler_params=LIMIT,
    )(scan_rows, scan_cols, cut, mine, arrived)
    from_above = lax.ppermute(down, "region", forward)
    from_below = lax.ppermute(up, "region", backward)
    rims = jnp.concatenate([from_above, from_below], axis=1).astype(jnp.float32)
    return (inner + rims)[None]


def solution(mesh):
    return jax.shard_map(
        shards,
        mesh=mesh,
        in_specs=(
            P("cuts", None, "region", None),
            P(),
            P("region", None, None),
            P(),
            P("region"),
            P("region"),
            P("region"),
        ),
        out_specs=P("cuts", None, "region", None),
        check_vma=False,
    )
```

```python
import functools
import jax
import jax.numpy as jnp
import numpy as np
from jax import lax
from jax.experimental import pallas as pl
from jax.experimental.pallas import tpu as pltpu
from jax.sharding import PartitionSpec as P

modulus_floor = 0.25
LANES = 128
SUBLANES = 8
VMEM = pl.BlockSpec(memory_space=pltpu.VMEM)
SMEM = pl.BlockSpec(memory_space=pltpu.SMEM)
LIMIT = pltpu.CompilerParams(vmem_limit_bytes=60000 * 1024)


def dft_blocks(side):
    indices = np.arange(side)
    angles = (indices[:, None] * indices[None, :] % side) * (2.0 * np.pi / side)
    real = np.cos(angles) / np.sqrt(side)
    imag = np.sin(angles) / np.sqrt(side)
    tables = []
    for sign in (-1.0, 1.0):
        tables.append(np.block([[real, -sign * imag], [sign * imag, real]]))
        tables.append(np.block([[real, sign * imag], [-sign * imag, real]]))
    return jnp.asarray(np.stack(tables), dtype=jnp.bfloat16)


def split_col(col, cols, side):
    base = jnp.minimum(lax.div(col, LANES), (cols - side) // LANES - 1) * LANES
    return base, col - base


def cut_window(ext, plane, row, col, height, side):
    base, shift = split_col(col, ext.shape[2], side)
    top = lax.div(row, SUBLANES) * SUBLANES
    tall = height + SUBLANES
    block = ext[plane, pl.ds(top, tall), pl.ds(base, side + LANES)]
    block = pltpu.roll(block, lax.rem(tall + top - row, tall), axis=0)[:height]
    back = lax.rem(LANES - shift + LANES, LANES)
    chunks = [
        pltpu.roll(block[:, j : j + LANES], back, axis=1) for j in range(0, side + LANES, LANES)
    ]
    lane = lax.broadcasted_iota(jnp.int32, (height, LANES), 1)
    keep = lane < LANES - shift
    return jnp.concatenate(
        [jnp.where(keep, chunks[j], chunks[j + 1]) for j in range(len(chunks) - 1)], axis=1
    )


def add_window(grad, plane, row, col, field):
    height, side = field.shape
    base, shift = split_col(col, grad.shape[2], side)
    top = lax.div(row, SUBLANES) * SUBLANES
    tall = height + SUBLANES
    field = jnp.concatenate([field, jnp.zeros((SUBLANES, side), field.dtype)], axis=0)
    field = pltpu.roll(field, row - top, axis=0)
    ahead = lax.rem(shift, LANES)
    chunks = [pltpu.roll(field[:, j : j + LANES], ahead, axis=1) for j in range(0, side, LANES)]
    lane = lax.broadcasted_iota(jnp.int32, (tall, LANES), 1)
    keep = lane >= shift
    zero = jnp.zeros((tall, LANES), field.dtype)
    parts = [zero] + chunks + [zero]
    placed = jnp.concatenate(
        [jnp.where(keep, parts[j + 1], parts[j]) for j in range(len(chunks) + 1)], axis=1
    )
    where = (plane, pl.ds(top, tall), pl.ds(base, side + LANES))
    grad[where] = grad[where] + placed


def dot(left, right):
    return jnp.dot(left, right, preferred_element_type=jnp.float32)


def transform(field, tables, which):
    side = field[0].shape[0]
    stacked = jnp.concatenate([field[0].astype(jnp.bfloat16), field[1].astype(jnp.bfloat16)], axis=0)
    middle = dot(tables[which], stacked).astype(jnp.bfloat16)
    beside = jnp.concatenate([middle[:side], middle[side:]], axis=1)
    result = dot(beside, tables[which + 1])
    return result[:, :side], result[:, side:]


def multiply(left, right):
    return left[0] * right[0] - left[1] * right[1], left[0] * right[1] + left[1] * right[0]


def multiply_conjugate(left, right):
    return left[0] * right[0] + left[1] * right[1], left[0] * right[1] - left[1] * right[0]


def narrowed(field):
    return tuple(part.astype(jnp.bfloat16).astype(jnp.float32) for part in field)


def one_position(psi0, object0, object1, measured, wave, tables):
    psi1 = narrowed(
        transform(multiply(wave, transform(multiply(psi0, object0), tables, 0)), tables, 2)
    )
    far = transform(multiply(psi1, object1), tables, 0)
    modulus = jnp.sqrt(far[0] * far[0] + far[1] * far[1])
    factor = 1.0 - measured / jnp.maximum(modulus, modulus_floor)
    g1 = narrowed(transform((far[0] * factor, far[1] * factor), tables, 2))
    d1 = multiply_conjugate(psi1, g1)
    back = transform(multiply_conjugate(object1, g1), tables, 0)
    g0 = narrowed(transform(multiply_conjugate(wave, back), tables, 2))
    return multiply_conjugate(psi0, g0), d1


def wide(ref, *index):
    return ref[index + (0,)].astype(jnp.float32), ref[index + (1,)].astype(jnp.float32)


def pick(info, kind, side_index, rank, values):
    seen = jnp.int32(0)
    chosen = jnp.int32(0)
    for position in range(info.shape[1]):
        above = info[0, position] < 0
        here = above if side_index == 0 else jnp.logical_not(above)
        match = jnp.logical_and(here, seen == rank)
        chosen = chosen + jnp.where(match, values(position), 0)
        seen = seen + jnp.where(here, 1, 0)
    return chosen


def corner(info, side_index, rank):
    row = pick(info, 0, side_index, rank, lambda position: info[0, position])
    col = pick(info, 1, side_index, rank, lambda position: info[1, position])
    return row, col


def near_rows(side_index, side):
    return (side // 4, side) if side_index == 0 else (0, side - side // 4)


def far_rows(side_index, side):
    return (0, side // 2) if side_index == 0 else (side // 2, side)


def wave_kernel(
    side, count, here, before, after, choice,
    band, probes_any, amps_any, wave_any, tables_any,
    mine, near_out, far_out,
    ext, probes, amps, wave, tables,
    near_send, far_send, near_in, far_in, near_back, far_back,
    local_sem, send_sem, recv_sem,
):
    rim = side // 2
    quarter = side // 4
    band_rows = band.shape[1]
    c = lax.axis_index("cuts")
    region = lax.axis_index("region")
    other_cut = 1 - c
    prior = lax.rem(region + count - 1, count)
    following = lax.rem(region + 1, count)
    loads = [
        pltpu.make_async_copy(source, target, local_sem.at[k])
        for k, (source, target) in enumerate((
            (band, ext.at[:, pl.ds(rim, band_rows)]),
            (probes_any, probes), (amps_any, amps), (wave_any, wave), (tables_any, tables),
        ))
    ]
    for load in loads:
        load.start()
    barrier = pltpu.get_barrier_semaphore()
    peers = [(other_cut, region)]
    peers += [(q, t) for q in (c, other_cut) for t in (prior, following)]
    for peer in peers:
        pl.semaphore_signal(barrier, 1, device_id=peer, device_id_type=pl.DeviceIdType.MESH)
    loads[0].wait()

    def remote(source, target, slot, peer):
        return pltpu.make_async_remote_copy(
            src_ref=source, dst_ref=target,
            send_sem=send_sem.at[slot], recv_sem=recv_sem.at[slot],
            device_id=peer, device_id_type=pl.DeviceIdType.MESH,
        )

    sends = [[], []]
    for d in range(2):
        row, col = corner(here, d, other_cut)
        low, high = near_rows(d, side)
        for plane in range(2):
            near_send[d, plane] = cut_window(
                ext, plane, row + rim + low, col, high - low, side
            ).astype(jnp.bfloat16)
        sends[d].append(remote(near_send.at[d], near_in.at[d], 6 * d, (other_cut, region)))
        if d == 0:
            pl.semaphore_wait(barrier, len(peers))
        sends[d][0].start()
        info, peer_region, offset = (
            (after, following, band_rows) if d == 0 else (before, prior, -band_rows)
        )
        low, high = far_rows(d, side)
        for j, q in enumerate((c, other_cut)):
            row, col = corner(info, d, q)
            for plane in range(2):
                far_send[d, j, plane] = cut_window(
                    ext, plane, row + rim + offset + low, col, high - low, side
                ).astype(jnp.bfloat16)
            copy = remote(far_send.at[d, j], far_in.at[d, j], 6 * d + 1 + j, (q, peer_region))
            copy.start()
            sends[d].append(copy)
    for load in loads[1:]:
        load.wait()
    first = c == 0
    backs = []
    ids = lax.broadcasted_iota(jnp.int32, (rim, side), 0)
    for d in range(2):
        position = pick(here, 0, d, c, lambda p: p)
        chosen = pick(here, 0, d, c, lambda p: choice[p])
        row, col = corner(here, d, c)
        psi0 = wide(probes, chosen)
        own = [cut_window(ext, plane, row + rim, col, side, side) for plane in range(2)]
        for copy in sends[d]:
            copy.wait_recv()
        other = []
        for plane in range(2):
            far = far_in[d, 0, plane].astype(jnp.float32)
            far_other = far_in[d, 1, plane].astype(jnp.float32)
            near_other = near_in[d, plane].astype(jnp.float32)
            near_own = own[plane]
            if d == 0:
                mixed = jnp.where(ids < -row, far, near_own[:rim])
                own[plane] = jnp.concatenate([mixed, near_own[rim:]], axis=0)
                mixed = jnp.where(ids[quarter:] < -row, far_other[quarter:], near_other[:quarter])
                parts = [far_other[:quarter], mixed, near_other[quarter:]]
            else:
                mixed = jnp.where(ids >= rim - row, far, near_own[rim:])
                own[plane] = jnp.concatenate([near_own[:rim], mixed], axis=0)
                mixed = jnp.where(ids[:quarter] >= rim - row, far_other[:quarter], near_other[rim:])
                parts = [near_other[:rim], mixed, far_other[quarter:]]
            other.append(jnp.concatenate(parts, axis=0))
        object0 = tuple(jnp.where(first, x, y) for x, y in zip(own, other))
        object1 = tuple(jnp.where(first, y, x) for x, y in zip(own, other))
        d0, d1 = one_position(psi0, object0, object1, amps[position], (wave[0], wave[1]), tables)
        peer_region = prior if d == 0 else following
        near_low, near_high = near_rows(d, side)
        low, high = far_rows(d, side)
        for plane in range(2):
            kept = jnp.where(first, d0[plane], d1[plane]).astype(jnp.bfloat16)
            given = jnp.where(first, d1[plane], d0[plane]).astype(jnp.bfloat16)
            mine[d, plane] = kept[near_low:near_high]
            near_back[d, plane] = given[near_low:near_high]
            far_back[d, 0, plane] = kept[low:high]
            far_back[d, 1, plane] = given[low:high]
        backs.append(remote(near_back.at[d], near_out.at[d], 6 * d + 3, (other_cut, region)))
        for j, q in enumerate((c, other_cut)):
            backs.append(
                remote(far_back.at[d, j], far_out.at[d, j], 6 * d + 4 + j, (q, peer_region))
            )
        for copy in backs[-3:]:
            copy.start()
    for copy in sends[0] + sends[1]:
        copy.wait_send()
    for copy in backs:
        copy.wait()


def deposit_kernel(side, here, before, after, cut, mine, near, far, out, grad):
    rim = side // 2
    band_rows = out.shape[1]
    c = cut[0]
    grad[...] = jnp.zeros_like(grad)
    for d in range(2):
        low, _ = near_rows(d, side)
        far_low, _ = far_rows(d, side)
        info, offset = (after, band_rows) if d == 0 else (before, -band_rows)
        parts = [
            (mine.at[d], here, c, rim + low),
            (near.at[d], here, 1 - c, rim + low),
            (far.at[d, 0], info, c, rim + offset + far_low),
            (far.at[d, 1], info, 1 - c, rim + offset + far_low),
        ]
        for source, table, rank, shift in parts:
            row, col = corner(table, d, rank)
            for plane in range(2):
                add_window(grad, plane, row + shift, col, source[plane].astype(jnp.float32))
    out[...] = grad[:, rim : rim + band_rows]


def shards(objects, probes, amplitudes, prop_phase, scan_rows, scan_cols, probe_choice):
    side = probes.shape[-1]
    rim = side // 2
    count = lax.axis_size("region")
    band = objects[0]
    band_rows, columns = band.shape[1:]
    cut = lax.axis_index("cuts").astype(jnp.int32)[None]
    here = jnp.stack([scan_rows, scan_cols])
    before = lax.ppermute(here, "region", [(i, (i + 1) % count) for i in range(count)])
    after = lax.ppermute(here, "region", [(i, (i - 1) % count) for i in range(count)])
    wave = jnp.stack([jnp.cos(prop_phase), jnp.sin(prop_phase)])
    tables = dft_blocks(side)
    near = (2, 2, side - side // 4, side)
    far = (2, 2, 2, rim, side)
    held = lambda shape: jax.ShapeDtypeStruct(shape, jnp.bfloat16)
    slot = lambda shape: pltpu.VMEM(shape, jnp.bfloat16)
    tall = pltpu.VMEM((2, band_rows + 2 * rim + SUBLANES, columns), jnp.float32)
    ANY = pl.BlockSpec(memory_space=pl.ANY)
    mine, near_part, far_part = pl.pallas_call(
        functools.partial(wave_kernel, side, count),
        out_shape=(held(near), held(near), held(far)),
        in_specs=[SMEM] * 4 + [ANY] * 5,
        out_specs=(VMEM, VMEM, VMEM),
        scratch_shapes=[
            tall,
            pltpu.VMEM(probes.shape, probes.dtype),
            pltpu.VMEM(amplitudes.shape, amplitudes.dtype),
            pltpu.VMEM(wave.shape, wave.dtype),
            pltpu.VMEM(tables.shape, tables.dtype),
            slot(near), slot(far), slot(near), slot(far), slot(near), slot(far),
            pltpu.SemaphoreType.DMA((5,)),
            pltpu.SemaphoreType.DMA((12,)),
            pltpu.SemaphoreType.DMA((12,)),
        ],
        compiler_params=pltpu.CompilerParams(
            collective_id=0, has_side_effects=True, vmem_limit_bytes=60000 * 1024
        ),
    )(here, before, after, probe_choice, band, probes, amplitudes, wave, tables)
    out = pl.pallas_call(
        functools.partial(deposit_kernel, side),
        out_shape=jax.ShapeDtypeStruct(band.shape, jnp.float32),
        in_specs=[SMEM] * 4 + [VMEM] * 3,
        out_specs=VMEM,
        scratch_shapes=[tall],
        compiler_params=LIMIT,
    )(here, before, after, cut, mine, near_part, far_part)
    return out[None]


def solution(mesh):
    return jax.shard_map(
        shards,
        mesh=mesh,
        in_specs=(
            P("cuts", None, "region", None),
            P(),
            P("region", None, None),
            P(),
            P("region"),
            P("region"),
            P("region"),
        ),
        out_specs=P("cuts", None, "region", None),
        check_vma=False,
    )
```

```python
import functools
import jax
import jax.numpy as jnp
import numpy as np
from jax import lax
from jax.experimental import pallas as pl
from jax.experimental.pallas import tpu as pltpu
from jax.sharding import PartitionSpec as P

modulus_floor = 0.25
LANES = 128
SUBLANES = 8
VMEM = pl.BlockSpec(memory_space=pltpu.VMEM)
SMEM = pl.BlockSpec(memory_space=pltpu.SMEM)
LIMIT = pltpu.CompilerParams(vmem_limit_bytes=60000 * 1024)


def dft_blocks(side):
    indices = np.arange(side)
    angles = (indices[:, None] * indices[None, :] % side) * (2.0 * np.pi / side)
    real = np.cos(angles) / np.sqrt(side)
    imag = np.sin(angles) / np.sqrt(side)
    tables = []
    for sign in (-1.0, 1.0):
        tables.append(np.block([[real, -sign * imag], [sign * imag, real]]))
        tables.append(np.block([[real, sign * imag], [-sign * imag, real]]))
    return jnp.asarray(np.stack(tables), dtype=jnp.bfloat16)


def split_col(col, cols, side):
    base = jnp.minimum(lax.div(col, LANES), (cols - side) // LANES - 1) * LANES
    return base, col - base


def cut_window(ext, plane, row, col, height, side):
    base, shift = split_col(col, ext.shape[2], side)
    top = lax.div(row, SUBLANES) * SUBLANES
    tall = height + SUBLANES
    block = ext[plane, pl.ds(top, tall), pl.ds(base, side + LANES)]
    block = pltpu.roll(block, lax.rem(tall + top - row, tall), axis=0)[:height]
    back = lax.rem(LANES - shift + LANES, LANES)
    chunks = [
        pltpu.roll(block[:, j : j + LANES], back, axis=1) for j in range(0, side + LANES, LANES)
    ]
    lane = lax.broadcasted_iota(jnp.int32, (height, LANES), 1)
    keep = lane < LANES - shift
    return jnp.concatenate(
        [jnp.where(keep, chunks[j], chunks[j + 1]) for j in range(len(chunks) - 1)], axis=1
    )


def add_window(grad, plane, row, col, field):
    height, side = field.shape
    base, shift = split_col(col, grad.shape[2], side)
    top = lax.div(row, SUBLANES) * SUBLANES
    tall = height + SUBLANES
    field = jnp.concatenate([field, jnp.zeros((SUBLANES, side), field.dtype)], axis=0)
    field = pltpu.roll(field, row - top, axis=0)
    ahead = lax.rem(shift, LANES)
    chunks = [pltpu.roll(field[:, j : j + LANES], ahead, axis=1) for j in range(0, side, LANES)]
    lane = lax.broadcasted_iota(jnp.int32, (tall, LANES), 1)
    keep = lane >= shift
    zero = jnp.zeros((tall, LANES), field.dtype)
    parts = [zero] + chunks + [zero]
    placed = jnp.concatenate(
        [jnp.where(keep, parts[j + 1], parts[j]) for j in range(len(chunks) + 1)], axis=1
    )
    where = (plane, pl.ds(top, tall), pl.ds(base, side + LANES))
    grad[where] = grad[where] + placed


def dot(left, right):
    return jnp.dot(left, right, preferred_element_type=jnp.float32)


def transform(field, tables, which):
    side = field[0].shape[0]
    stacked = jnp.concatenate([field[0].astype(jnp.bfloat16), field[1].astype(jnp.bfloat16)], axis=0)
    middle = dot(tables[which], stacked).astype(jnp.bfloat16)
    beside = jnp.concatenate([middle[:side], middle[side:]], axis=1)
    result = dot(beside, tables[which + 1])
    return result[:, :side], result[:, side:]


def multiply(left, right):
    return left[0] * right[0] - left[1] * right[1], left[0] * right[1] + left[1] * right[0]


def multiply_conjugate(left, right):
    return left[0] * right[0] + left[1] * right[1], left[0] * right[1] - left[1] * right[0]


def narrowed(field):
    return tuple(part.astype(jnp.bfloat16).astype(jnp.float32) for part in field)


def one_position(psi0, object0, object1, measured, wave, tables):
    psi1 = narrowed(
        transform(multiply(wave, transform(multiply(psi0, object0), tables, 0)), tables, 2)
    )
    far = transform(multiply(psi1, object1), tables, 0)
    modulus = jnp.sqrt(far[0] * far[0] + far[1] * far[1])
    factor = 1.0 - measured / jnp.maximum(modulus, modulus_floor)
    g1 = narrowed(transform((far[0] * factor, far[1] * factor), tables, 2))
    d1 = multiply_conjugate(psi1, g1)
    back = transform(multiply_conjugate(object1, g1), tables, 0)
    g0 = narrowed(transform(multiply_conjugate(wave, back), tables, 2))
    return multiply_conjugate(psi0, g0), d1


def wide(ref, *index):
    return ref[index + (0,)].astype(jnp.float32), ref[index + (1,)].astype(jnp.float32)


def pick(info, kind, side_index, rank, values):
    seen = jnp.int32(0)
    chosen = jnp.int32(0)
    for position in range(info[0].shape[0]):
        above = info[0][position] < 0
        here = above if side_index == 0 else jnp.logical_not(above)
        match = jnp.logical_and(here, seen == rank)
        chosen = chosen + jnp.where(match, values(position), 0)
        seen = seen + jnp.where(here, 1, 0)
    return chosen


def corner(info, side_index, rank):
    row = pick(info, 0, side_index, rank, lambda position: info[0][position])
    col = pick(info, 1, side_index, rank, lambda position: info[1][position])
    return row, col


def near_rows(side_index, side):
    return (side // 4, side) if side_index == 0 else (0, side - side // 4)


def far_rows(side_index, side):
    return (0, side // 2) if side_index == 0 else (side // 2, side)


def wave_kernel(
    side, count, scans, choice_any, band, probes_any, amps_any, phase_any, tables_any,
    mine, near_out, far_out, around,
    ext, probes, amps, phase, wave, tables,
    near_send, far_send, near_in, far_in, near_back, far_back, here, before, after, choice,
    local_sem, info_sem, send_sem, recv_sem,
):
    rim = side // 2
    quarter = side // 4
    band_rows = band.shape[1]
    c = lax.axis_index("cuts")
    region = lax.axis_index("region")
    other_cut = 1 - c
    prior = lax.rem(region + count - 1, count)
    following = lax.rem(region + 1, count)
    loads = [
        pltpu.make_async_copy(source, target, local_sem.at[k])
        for k, (source, target) in enumerate((
            (scans[0], here[0]), (scans[1], here[1]), (choice_any, choice),
            (band, ext.at[:, pl.ds(rim, band_rows)]), (phase_any, phase),
            (tables_any, tables), (probes_any, probes), (amps_any, amps),
        ))
    ]
    for load in loads:
        load.start()
    barrier = pltpu.get_barrier_semaphore()
    peers = [(other_cut, region)]
    peers += [(q, t) for q in (c, other_cut) for t in (prior, following)]
    for peer in peers:
        pl.semaphore_signal(barrier, 1, device_id=peer, device_id_type=pl.DeviceIdType.MESH)
    pl.semaphore_wait(barrier, len(peers))

    def remote(source, target, slot, peer):
        return pltpu.make_async_remote_copy(
            src_ref=source, dst_ref=target,
            send_sem=send_sem.at[slot], recv_sem=recv_sem.at[slot],
            device_id=peer, device_id_type=pl.DeviceIdType.MESH,
        )

    notes = []
    for k, (source, target) in enumerate(zip(scans + scans, around)):
        notes.append(remote(source, target, 12 + k, (c, following if k < 2 else prior)))
        notes[-1].start()
    for load in loads[:4]:
        load.wait()
    sends = [[], []]
    for d in range(2):
        row, col = corner(here, d, other_cut)
        low, high = near_rows(d, side)
        for plane in range(2):
            near_send[d, plane] = cut_window(
                ext, plane, row + rim + low, col, high - low, side
            ).astype(jnp.bfloat16)
        sends[d].append(remote(near_send.at[d], near_in.at[d], 6 * d, (other_cut, region)))
        sends[d][0].start()
        if d == 0:
            fetches = []
            for k, target in enumerate(before + after):
                notes[k].wait()
                fetches.append(pltpu.make_async_copy(around[k], target, info_sem.at[k]))
                fetches[-1].start()
            for fetch in fetches:
                fetch.wait()
        info, peer_region, offset = (
            (after, following, band_rows) if d == 0 else (before, prior, -band_rows)
        )
        low, high = far_rows(d, side)
        for j, q in enumerate((c, other_cut)):
            row, col = corner(info, d, q)
            for plane in range(2):
                far_send[d, j, plane] = cut_window(
                    ext, plane, row + rim + offset + low, col, high - low, side
                ).astype(jnp.bfloat16)
            copy = remote(far_send.at[d, j], far_in.at[d, j], 6 * d + 1 + j, (q, peer_region))
            copy.start()
            sends[d].append(copy)
    for load in loads[4:]:
        load.wait()
    wave[0] = jnp.cos(phase[...])
    wave[1] = jnp.sin(phase[...])
    first = c == 0
    backs = []
    ids = lax.broadcasted_iota(jnp.int32, (rim, side), 0)
    for d in range(2):
        position = pick(here, 0, d, c, lambda p: p)
        chosen = pick(here, 0, d, c, lambda p: choice[p])
        row, col = corner(here, d, c)
        psi0 = wide(probes, chosen)
        own = [cut_window(ext, plane, row + rim, col, side, side) for plane in range(2)]
        for copy in sends[d]:
            copy.wait_recv()
        other = []
        for plane in range(2):
            far = far_in[d, 0, plane].astype(jnp.float32)
            far_other = far_in[d, 1, plane].astype(jnp.float32)
            near_other = near_in[d, plane].astype(jnp.float32)
            near_own = own[plane]
            if d == 0:
                mixed = jnp.where(ids < -row, far, near_own[:rim])
                own[plane] = jnp.concatenate([mixed, near_own[rim:]], axis=0)
                mixed = jnp.where(ids[quarter:] < -row, far_other[quarter:], near_other[:quarter])
                parts = [far_other[:quarter], mixed, near_other[quarter:]]
            else:
                mixed = jnp.where(ids >= rim - row, far, near_own[rim:])
                own[plane] = jnp.concatenate([near_own[:rim], mixed], axis=0)
                mixed = jnp.where(ids[:quarter] >= rim - row, far_other[:quarter], near_other[rim:])
                parts = [near_other[:rim], mixed, far_other[quarter:]]
            other.append(jnp.concatenate(parts, axis=0))
        object0 = tuple(jnp.where(first, x, y) for x, y in zip(own, other))
        object1 = tuple(jnp.where(first, y, x) for x, y in zip(own, other))
        d0, d1 = one_position(psi0, object0, object1, amps[position], (wave[0], wave[1]), tables)
        peer_region = prior if d == 0 else following
        near_low, near_high = near_rows(d, side)
        low, high = far_rows(d, side)
        for plane in range(2):
            kept = jnp.where(first, d0[plane], d1[plane]).astype(jnp.bfloat16)
            given = jnp.where(first, d1[plane], d0[plane]).astype(jnp.bfloat16)
            mine[d, plane] = kept[near_low:near_high]
            near_back[d, plane] = given[near_low:near_high]
            far_back[d, 0, plane] = kept[low:high]
            far_back[d, 1, plane] = given[low:high]
        backs.append(remote(near_back.at[d], near_out.at[d], 6 * d + 3, (other_cut, region)))
        for j, q in enumerate((c, other_cut)):
            backs.append(
                remote(far_back.at[d, j], far_out.at[d, j], 6 * d + 4 + j, (q, peer_region))
            )
        for copy in backs[-3:]:
            copy.start()
    for copy in sends[0] + sends[1]:
        copy.wait_send()
    for copy in backs:
        copy.wait()


def deposit_kernel(
    side, scans, around, mine, near, far, out, grad, here, before, after, local_sem, out_sem
):
    rim = side // 2
    band_rows = out.shape[1]
    c = lax.axis_index("cuts")
    loads = [
        pltpu.make_async_copy(source, target, local_sem.at[k])
        for k, (source, target) in enumerate(zip(scans + around, here + before + after))
    ]
    for load in loads:
        load.start()
    grad[...] = jnp.zeros_like(grad)
    for load in loads:
        load.wait()
    stores = []
    for plane in range(2):
        for d in range(2):
            low, _ = near_rows(d, side)
            far_low, _ = far_rows(d, side)
            info, offset = (after, band_rows) if d == 0 else (before, -band_rows)
            parts = [
                (mine.at[d], here, c, rim + low),
                (near.at[d], here, 1 - c, rim + low),
                (far.at[d, 0], info, c, rim + offset + far_low),
                (far.at[d, 1], info, 1 - c, rim + offset + far_low),
            ]
            for source, table, rank, shift in parts:
                row, col = corner(table, d, rank)
                add_window(grad, plane, row + shift, col, source[plane].astype(jnp.float32))
        stores.append(
            pltpu.make_async_copy(
                grad.at[plane, pl.ds(rim, band_rows)], out.at[plane], out_sem.at[plane]
            )
        )
        stores[-1].start()
    for store in stores:
        store.wait()


def shards(objects, probes, amplitudes, prop_phase, scan_rows, scan_cols, probe_choice):
    side = probes.shape[-1]
    rim = side // 2
    count = lax.axis_size("region")
    band = objects[0]
    band_rows, columns = band.shape[1:]
    tables = dft_blocks(side)
    near = (2, 2, side - side // 4, side)
    far = (2, 2, 2, rim, side)
    held = lambda shape: jax.ShapeDtypeStruct(shape, jnp.bfloat16)
    slot = lambda shape: pltpu.VMEM(shape, jnp.bfloat16)
    tall = pltpu.VMEM((2, band_rows + 2 * rim + SUBLANES, columns), jnp.float32)
    ANY = pl.BlockSpec(memory_space=pl.ANY)
    scans = (scan_rows, scan_cols)
    info = jax.ShapeDtypeStruct(scan_rows.shape, jnp.int32)
    scalars = pltpu.SMEM(scan_rows.shape, jnp.int32)
    mine, near_part, far_part, around = pl.pallas_call(
        functools.partial(wave_kernel, side, count),
        out_shape=(held(near), held(near), held(far), (info,) * 4),
        in_specs=[(ANY, ANY)] + [ANY] * 6,
        out_specs=(VMEM, VMEM, VMEM, (ANY,) * 4),
        scratch_shapes=[
            tall,
            pltpu.VMEM(probes.shape, probes.dtype),
            pltpu.VMEM(amplitudes.shape, amplitudes.dtype),
            pltpu.VMEM(prop_phase.shape, jnp.float32),
            pltpu.VMEM((2,) + prop_phase.shape, jnp.float32),
            pltpu.VMEM(tables.shape, tables.dtype),
            slot(near), slot(far), slot(near), slot(far), slot(near), slot(far),
            (scalars,) * 2, (scalars,) * 2, (scalars,) * 2, scalars,
            pltpu.SemaphoreType.DMA((8,)),
            pltpu.SemaphoreType.DMA((4,)),
            pltpu.SemaphoreType.DMA((16,)),
            pltpu.SemaphoreType.DMA((16,)),
        ],
        compiler_params=pltpu.CompilerParams(
            collective_id=0, has_side_effects=True, vmem_limit_bytes=60000 * 1024
        ),
    )(scans, probe_choice, band, probes, amplitudes, prop_phase, tables)
    out = pl.pallas_call(
        functools.partial(deposit_kernel, side),
        out_shape=jax.ShapeDtypeStruct(band.shape, jnp.float32),
        in_specs=[(ANY, ANY), (ANY,) * 4] + [VMEM] * 3,
        out_specs=ANY,
        scratch_shapes=[
            tall, (scalars,) * 2, (scalars,) * 2, (scalars,) * 2,
            pltpu.SemaphoreType.DMA((6,)),
            pltpu.SemaphoreType.DMA((2,)),
        ],
        compiler_params=LIMIT,
    )(scans, around, mine, near_part, far_part)
    return out[None]


def solution(mesh):
    return jax.shard_map(
        shards,
        mesh=mesh,
        in_specs=(
            P("cuts", None, "region", None),
            P(),
            P("region", None, None),
            P(),
            P("region"),
            P("region"),
            P("region"),
        ),
        out_specs=P("cuts", None, "region", None),
        check_vma=False,
    )
```

```python
import functools
import jax
import jax.numpy as jnp
import numpy as np
from jax import lax
from jax.experimental import pallas as pl
from jax.experimental.pallas import tpu as pltpu
from jax.sharding import PartitionSpec as P

modulus_floor = 0.25
LANES = 128
SUBLANES = 8
VMEM = pl.BlockSpec(memory_space=pltpu.VMEM)
SMEM = pl.BlockSpec(memory_space=pltpu.SMEM)
LIMIT = pltpu.CompilerParams(vmem_limit_bytes=60000 * 1024)


def dft_blocks(side):
    indices = np.arange(side)
    angles = (indices[:, None] * indices[None, :] % side) * (2.0 * np.pi / side)
    real = np.cos(angles) / np.sqrt(side)
    imag = np.sin(angles) / np.sqrt(side)
    tables = []
    for sign in (-1.0, 1.0):
        tables.append(np.block([[real, -sign * imag], [sign * imag, real]]))
        tables.append(np.block([[real, sign * imag], [-sign * imag, real]]))
    return jnp.asarray(np.stack(tables), dtype=jnp.bfloat16)


def split_col(col, cols, side):
    base = jnp.minimum(lax.div(col, LANES), (cols - side) // LANES - 1) * LANES
    return base, col - base


def cut_window(ext, plane, row, col, height, side):
    base, shift = split_col(col, ext.shape[2], side)
    top = lax.div(row, SUBLANES) * SUBLANES
    tall = height + SUBLANES
    block = ext[plane, pl.ds(top, tall), pl.ds(base, side + LANES)]
    block = pltpu.roll(block, lax.rem(tall + top - row, tall), axis=0)[:height]
    back = lax.rem(LANES - shift + LANES, LANES)
    chunks = [
        pltpu.roll(block[:, j : j + LANES], back, axis=1) for j in range(0, side + LANES, LANES)
    ]
    lane = lax.broadcasted_iota(jnp.int32, (height, LANES), 1)
    keep = lane < LANES - shift
    return jnp.concatenate(
        [jnp.where(keep, chunks[j], chunks[j + 1]) for j in range(len(chunks) - 1)], axis=1
    )


def add_window(grad, plane, row, col, field):
    height, side = field.shape
    base, shift = split_col(col, grad.shape[2], side)
    top = lax.div(row, SUBLANES) * SUBLANES
    tall = height + SUBLANES
    field = jnp.concatenate([field, jnp.zeros((SUBLANES, side), field.dtype)], axis=0)
    field = pltpu.roll(field, row - top, axis=0)
    ahead = lax.rem(shift, LANES)
    chunks = [pltpu.roll(field[:, j : j + LANES], ahead, axis=1) for j in range(0, side, LANES)]
    lane = lax.broadcasted_iota(jnp.int32, (tall, LANES), 1)
    keep = lane >= shift
    zero = jnp.zeros((tall, LANES), field.dtype)
    parts = [zero] + chunks + [zero]
    placed = jnp.concatenate(
        [jnp.where(keep, parts[j + 1], parts[j]) for j in range(len(chunks) + 1)], axis=1
    )
    where = (plane, pl.ds(top, tall), pl.ds(base, side + LANES))
    grad[where] = grad[where] + placed


def dot(left, right):
    return jnp.dot(left, right, preferred_element_type=jnp.float32)


def transform(field, tables, which):
    side = field[0].shape[0]
    stacked = jnp.concatenate([field[0].astype(jnp.bfloat16), field[1].astype(jnp.bfloat16)], axis=0)
    middle = dot(tables[which], stacked).astype(jnp.bfloat16)
    beside = jnp.concatenate([middle[:side], middle[side:]], axis=1)
    result = dot(beside, tables[which + 1])
    return result[:, :side], result[:, side:]


def multiply(left, right):
    return left[0] * right[0] - left[1] * right[1], left[0] * right[1] + left[1] * right[0]


def multiply_conjugate(left, right):
    return left[0] * right[0] + left[1] * right[1], left[0] * right[1] - left[1] * right[0]


def narrowed(field):
    return tuple(part.astype(jnp.bfloat16).astype(jnp.float32) for part in field)


def one_position(psi0, object0, object1, measured, wave, tables):
    psi1 = narrowed(
        transform(multiply(wave, transform(multiply(psi0, object0), tables, 0)), tables, 2)
    )
    far = transform(multiply(psi1, object1), tables, 0)
    modulus = jnp.sqrt(far[0] * far[0] + far[1] * far[1])
    factor = 1.0 - measured / jnp.maximum(modulus, modulus_floor)
    g1 = narrowed(transform((far[0] * factor, far[1] * factor), tables, 2))
    d1 = multiply_conjugate(psi1, g1)
    back = transform(multiply_conjugate(object1, g1), tables, 0)
    g0 = narrowed(transform(multiply_conjugate(wave, back), tables, 2))
    return multiply_conjugate(psi0, g0), d1


def wide(ref, *index):
    return ref[index + (0,)].astype(jnp.float32), ref[index + (1,)].astype(jnp.float32)


def pick(info, kind, side_index, rank, values):
    seen = jnp.int32(0)
    chosen = jnp.int32(0)
    for position in range(info[0].shape[0]):
        above = info[0][position] < 0
        here = above if side_index == 0 else jnp.logical_not(above)
        match = jnp.logical_and(here, seen == rank)
        chosen = chosen + jnp.where(match, values(position), 0)
        seen = seen + jnp.where(here, 1, 0)
    return chosen


def corner(info, side_index, rank):
    row = pick(info, 0, side_index, rank, lambda position: info[0][position])
    col = pick(info, 1, side_index, rank, lambda position: info[1][position])
    return row, col


def near_rows(side_index, side):
    return (side // 4, side) if side_index == 0 else (0, side - side // 4)


def far_rows(side_index, side):
    return (0, side // 2) if side_index == 0 else (side // 2, side)


def wave_kernel(
    side, count, scans, choice_any, band, probes_any, amps_any, phase_any, tables_any,
    mine, full_out, near_out, far_out, around,
    ext, probes, amps, phase, wave, tables,
    near_send, far_send, near_in, far_in, full_back, near_back, far_back, here, before, after, choice,
    local_sem, info_sem, send_sem, recv_sem,
):
    rim = side // 2
    quarter = side // 4
    band_rows = band.shape[1]
    c = lax.axis_index("cuts")
    region = lax.axis_index("region")
    other_cut = 1 - c
    prior = lax.rem(region + count - 1, count)
    following = lax.rem(region + 1, count)
    loads = [
        pltpu.make_async_copy(source, target, local_sem.at[k])
        for k, (source, target) in enumerate((
            (scans[0], here[0]), (scans[1], here[1]), (choice_any, choice),
            (band, ext.at[:, pl.ds(rim, band_rows)]), (phase_any, phase),
            (tables_any, tables), (probes_any, probes), (amps_any, amps),
        ))
    ]
    for load in loads:
        load.start()
    barrier = pltpu.get_barrier_semaphore()
    peers = [(other_cut, region)]
    peers += [(q, t) for q in (c, other_cut) for t in (prior, following)]
    for peer in peers:
        pl.semaphore_signal(barrier, 1, device_id=peer, device_id_type=pl.DeviceIdType.MESH)

    def remote(source, target, slot, peer):
        return pltpu.make_async_remote_copy(
            src_ref=source, dst_ref=target,
            send_sem=send_sem.at[slot], recv_sem=recv_sem.at[slot],
            device_id=peer, device_id_type=pl.DeviceIdType.MESH,
        )

    for load in loads[:4]:
        load.wait()
    for d in range(2):
        row, col = corner(here, d, other_cut)
        low, high = near_rows(d, side)
        for plane in range(2):
            near_send[d, plane] = cut_window(
                ext, plane, row + rim + low, col, high - low, side
            ).astype(jnp.bfloat16)
    pl.semaphore_wait(barrier, len(peers))
    notes = []
    for k, (source, target) in enumerate(zip(scans + scans, around)):
        notes.append(remote(source, target, 12 + k, (c, following if k < 2 else prior)))
        notes[-1].start()
    sends = [[], []]
    for d in range(2):
        sends[d].append(remote(near_send.at[d], near_in.at[d], 6 * d, (other_cut, region)))
        sends[d][0].start()
        if d == 0:
            fetches = []
            for k, target in enumerate(before + after):
                notes[k].wait()
                fetches.append(pltpu.make_async_copy(around[k], target, info_sem.at[k]))
                fetches[-1].start()
            for fetch in fetches:
                fetch.wait()
        info, peer_region, offset = (
            (after, following, band_rows) if d == 0 else (before, prior, -band_rows)
        )
        low, high = far_rows(d, side)
        for j, q in enumerate((c, other_cut)):
            row, col = corner(info, d, q)
            for plane in range(2):
                far_send[d, j, plane] = cut_window(
                    ext, plane, row + rim + offset + low, col, high - low, side
                ).astype(jnp.bfloat16)
            copy = remote(far_send.at[d, j], far_in.at[d, j], 6 * d + 1 + j, (q, peer_region))
            copy.start()
            sends[d].append(copy)
    for load in loads[4:]:
        load.wait()
    wave[0] = jnp.cos(phase[...])
    wave[1] = jnp.sin(phase[...])
    first = c == 0
    backs = []
    ids = lax.broadcasted_iota(jnp.int32, (rim, side), 0)
    for d in range(2):
        position = pick(here, 0, d, c, lambda p: p)
        chosen = pick(here, 0, d, c, lambda p: choice[p])
        row, col = corner(here, d, c)
        psi0 = wide(probes, chosen)
        own = [cut_window(ext, plane, row + rim, col, side, side) for plane in range(2)]
        for copy in sends[d]:
            copy.wait_recv()
        other = []
        for plane in range(2):
            far = far_in[d, 0, plane].astype(jnp.float32)
            far_other = far_in[d, 1, plane].astype(jnp.float32)
            near_other = near_in[d, plane].astype(jnp.float32)
            near_own = own[plane]
            if d == 0:
                mixed = jnp.where(ids < -row, far, near_own[:rim])
                own[plane] = jnp.concatenate([mixed, near_own[rim:]], axis=0)
                mixed = jnp.where(ids[quarter:] < -row, far_other[quarter:], near_other[:quarter])
                parts = [far_other[:quarter], mixed, near_other[quarter:]]
            else:
                mixed = jnp.where(ids >= rim - row, far, near_own[rim:])
                own[plane] = jnp.concatenate([near_own[:rim], mixed], axis=0)
                mixed = jnp.where(ids[:quarter] >= rim - row, far_other[:quarter], near_other[rim:])
                parts = [near_other[:rim], mixed, far_other[quarter:]]
            other.append(jnp.concatenate(parts, axis=0))
        object0 = tuple(jnp.where(first, x, y) for x, y in zip(own, other))
        object1 = tuple(jnp.where(first, y, x) for x, y in zip(own, other))
        d0, d1 = one_position(psi0, object0, object1, amps[position], (wave[0], wave[1]), tables)
        peer_region = prior if d == 0 else following
        near_low, near_high = near_rows(d, side)
        low, high = far_rows(d, side)
        for plane in range(2):
            kept = jnp.where(first, d0[plane], d1[plane]).astype(jnp.bfloat16)
            given = jnp.where(first, d1[plane], d0[plane]).astype(jnp.bfloat16)
            mine[d, plane] = kept[near_low:near_high]
            far_back[d, 0, plane] = kept[low:high]
            if d == 0:
                full_back[plane] = given
            else:
                near_back[plane] = given[near_low:near_high]
                far_back[d, 1, plane] = given[low:high]
        if d == 0:
            full = remote(full_back, full_out, 3, (other_cut, region))
            full.start()
        else:
            backs.append(
                remote(far_back.at[d, 1], far_out.at[d, 1], 11, (other_cut, peer_region))
            )
            backs[-1].start()
        backs.append(remote(far_back.at[d, 0], far_out.at[d, 0], 6 * d + 4, (c, peer_region)))
        backs[-1].start()
        if d == 1:
            backs.append(remote(near_back, near_out, 9, (other_cut, region)))
            backs[-1].start()
    full.wait()
    relay = remote(full_out.at[:, pl.ds(0, rim)], far_out.at[0, 1], 5, (c, prior))
    relay.start()
    backs.append(relay)
    for copy in sends[0] + sends[1]:
        copy.wait_send()
    for copy in backs:
        copy.wait()


def deposit_kernel(
    side, scans, around, mine, full, near, far, out, grad, here, before, after, local_sem, out_sem
):
    rim = side // 2
    band_rows = out.shape[1]
    c = lax.axis_index("cuts")
    loads = [
        pltpu.make_async_copy(source, target, local_sem.at[k])
        for k, (source, target) in enumerate(zip(scans + around, here + before + after))
    ]
    for load in loads:
        load.start()
    grad[...] = jnp.zeros_like(grad)
    for load in loads:
        load.wait()
    stores = []
    for plane in range(2):
        for d in range(2):
            low, _ = near_rows(d, side)
            far_low, _ = far_rows(d, side)
            info, offset = (after, band_rows) if d == 0 else (before, -band_rows)
            parts = [
                (mine.at[d], here, c, rim + low),
                (full.at[:, pl.ds(low, side - low)] if d == 0 else near, here, 1 - c, rim + low),
                (far.at[d, 0], info, c, rim + offset + far_low),
                (far.at[d, 1], info, 1 - c, rim + offset + far_low),
            ]
            for source, table, rank, shift in parts:
                row, col = corner(table, d, rank)
                add_window(grad, plane, row + shift, col, source[plane].astype(jnp.float32))
        stores.append(
            pltpu.make_async_copy(
                grad.at[plane, pl.ds(rim, band_rows)], out.at[plane], out_sem.at[plane]
            )
        )
        stores[-1].start()
    for store in stores:
        store.wait()


def shards(objects, probes, amplitudes, prop_phase, scan_rows, scan_cols, probe_choice):
    side = probes.shape[-1]
    rim = side // 2
    count = lax.axis_size("region")
    band = objects[0]
    band_rows, columns = band.shape[1:]
    tables = dft_blocks(side)
    near = (2, 2, side - side // 4, side)
    far = (2, 2, 2, rim, side)
    full = (2, side, side)
    held = lambda shape: jax.ShapeDtypeStruct(shape, jnp.bfloat16)
    slot = lambda shape: pltpu.VMEM(shape, jnp.bfloat16)
    tall = pltpu.VMEM((2, band_rows + 2 * rim + SUBLANES, columns), jnp.float32)
    ANY = pl.BlockSpec(memory_space=pl.ANY)
    scans = (scan_rows, scan_cols)
    info = jax.ShapeDtypeStruct(scan_rows.shape, jnp.int32)
    scalars = pltpu.SMEM(scan_rows.shape, jnp.int32)
    mine, full_part, near_part, far_part, around = pl.pallas_call(
        functools.partial(wave_kernel, side, count),
        out_shape=(held(near), held(full), held(near[1:]), held(far), (info,) * 4),
        in_specs=[(ANY, ANY)] + [ANY] * 6,
        out_specs=(VMEM, VMEM, VMEM, VMEM, (ANY,) * 4),
        scratch_shapes=[
            tall,
            pltpu.VMEM(probes.shape, probes.dtype),
            pltpu.VMEM(amplitudes.shape, amplitudes.dtype),
            pltpu.VMEM(prop_phase.shape, jnp.float32),
            pltpu.VMEM((2,) + prop_phase.shape, jnp.float32),
            pltpu.VMEM(tables.shape, tables.dtype),
            slot(near), slot(far), slot(near), slot(far), slot(full), slot(near[1:]), slot(far),
            (scalars,) * 2, (scalars,) * 2, (scalars,) * 2, scalars,
            pltpu.SemaphoreType.DMA((8,)),
            pltpu.SemaphoreType.DMA((4,)),
            pltpu.SemaphoreType.DMA((16,)),
            pltpu.SemaphoreType.DMA((16,)),
        ],
        compiler_params=pltpu.CompilerParams(
            collective_id=0, has_side_effects=True, vmem_limit_bytes=60000 * 1024
        ),
    )(scans, probe_choice, band, probes, amplitudes, prop_phase, tables)
    out = pl.pallas_call(
        functools.partial(deposit_kernel, side),
        out_shape=jax.ShapeDtypeStruct(band.shape, jnp.float32),
        in_specs=[(ANY, ANY), (ANY,) * 4] + [VMEM] * 4,
        out_specs=ANY,
        scratch_shapes=[
            tall, (scalars,) * 2, (scalars,) * 2, (scalars,) * 2,
            pltpu.SemaphoreType.DMA((6,)),
            pltpu.SemaphoreType.DMA((2,)),
        ],
        compiler_params=LIMIT,
    )(scans, around, mine, full_part, near_part, far_part)
    return out[None]


def solution(mesh):
    return jax.shard_map(
        shards,
        mesh=mesh,
        in_specs=(
            P("cuts", None, "region", None),
            P(),
            P("region", None, None),
            P(),
            P("region"),
            P("region"),
            P("region"),
        ),
        out_specs=P("cuts", None, "region", None),
        check_vma=False,
    )
```

```python
import functools
import jax
import jax.numpy as jnp
import numpy as np
from jax import lax
from jax.experimental import pallas as pl
from jax.experimental.pallas import tpu as pltpu
from jax.sharding import PartitionSpec as P

modulus_floor = 0.25
LANES = 128
SUBLANES = 8
VMEM = pl.BlockSpec(memory_space=pltpu.VMEM)
SMEM = pl.BlockSpec(memory_space=pltpu.SMEM)
LIMIT = pltpu.CompilerParams(vmem_limit_bytes=60000 * 1024)


def dft_blocks(side):
    indices = np.arange(side)
    angles = (indices[:, None] * indices[None, :] % side) * (2.0 * np.pi / side)
    real = np.cos(angles) / np.sqrt(side)
    imag = np.sin(angles) / np.sqrt(side)
    tables = []
    for sign in (-1.0, 1.0):
        tables.append(np.block([[real, -sign * imag], [sign * imag, real]]))
        tables.append(np.block([[real, sign * imag], [-sign * imag, real]]))
    return jnp.asarray(np.stack(tables), dtype=jnp.bfloat16)


def split_col(col, cols, side):
    base = jnp.minimum(lax.div(col, LANES), (cols - side) // LANES - 1) * LANES
    return base, col - base


def cut_window(ext, plane, row, col, height, side):
    base, shift = split_col(col, ext.shape[2], side)
    top = lax.div(row, SUBLANES) * SUBLANES
    tall = height + SUBLANES
    block = ext[plane, pl.ds(top, tall), pl.ds(base, side + LANES)]
    block = pltpu.roll(block, lax.rem(tall + top - row, tall), axis=0)[:height]
    back = lax.rem(LANES - shift + LANES, LANES)
    chunks = [
        pltpu.roll(block[:, j : j + LANES], back, axis=1) for j in range(0, side + LANES, LANES)
    ]
    lane = lax.broadcasted_iota(jnp.int32, (height, LANES), 1)
    keep = lane < LANES - shift
    return jnp.concatenate(
        [jnp.where(keep, chunks[j], chunks[j + 1]) for j in range(len(chunks) - 1)], axis=1
    )


def add_window(grad, plane, row, col, field):
    height, side = field.shape
    base, shift = split_col(col, grad.shape[2], side)
    top = lax.div(row, SUBLANES) * SUBLANES
    tall = height + SUBLANES
    field = jnp.concatenate([field, jnp.zeros((SUBLANES, side), field.dtype)], axis=0)
    field = pltpu.roll(field, row - top, axis=0)
    ahead = lax.rem(shift, LANES)
    chunks = [pltpu.roll(field[:, j : j + LANES], ahead, axis=1) for j in range(0, side, LANES)]
    lane = lax.broadcasted_iota(jnp.int32, (tall, LANES), 1)
    keep = lane >= shift
    zero = jnp.zeros((tall, LANES), field.dtype)
    parts = [zero] + chunks + [zero]
    placed = jnp.concatenate(
        [jnp.where(keep, parts[j + 1], parts[j]) for j in range(len(chunks) + 1)], axis=1
    )
    where = (plane, pl.ds(top, tall), pl.ds(base, side + LANES))
    grad[where] = grad[where] + placed


def dot(left, right):
    return jnp.dot(left, right, preferred_element_type=jnp.float32)


def transform(field, tables, which):
    side = field[0].shape[0]
    stacked = jnp.concatenate([field[0].astype(jnp.bfloat16), field[1].astype(jnp.bfloat16)], axis=0)
    middle = dot(tables[which], stacked).astype(jnp.bfloat16)
    beside = jnp.concatenate([middle[:side], middle[side:]], axis=1)
    result = dot(beside, tables[which + 1])
    return result[:, :side], result[:, side:]


def multiply(left, right):
    return left[0] * right[0] - left[1] * right[1], left[0] * right[1] + left[1] * right[0]


def multiply_conjugate(left, right):
    return left[0] * right[0] + left[1] * right[1], left[0] * right[1] - left[1] * right[0]


def narrowed(field):
    return tuple(part.astype(jnp.bfloat16).astype(jnp.float32) for part in field)


def one_position(psi0, object0, object1, measured, wave, tables):
    psi1 = narrowed(
        transform(multiply(wave, transform(multiply(psi0, object0), tables, 0)), tables, 2)
    )
    far = transform(multiply(psi1, object1), tables, 0)
    modulus = jnp.sqrt(far[0] * far[0] + far[1] * far[1])
    factor = 1.0 - measured / jnp.maximum(modulus, modulus_floor)
    g1 = narrowed(transform((far[0] * factor, far[1] * factor), tables, 2))
    d1 = multiply_conjugate(psi1, g1)
    back = transform(multiply_conjugate(object1, g1), tables, 0)
    g0 = narrowed(transform(multiply_conjugate(wave, back), tables, 2))
    return multiply_conjugate(psi0, g0), d1


def wide(ref, *index):
    return ref[index + (0,)].astype(jnp.float32), ref[index + (1,)].astype(jnp.float32)


def pick(info, kind, side_index, rank, values):
    seen = jnp.int32(0)
    chosen = jnp.int32(0)
    for position in range(info[0].shape[0]):
        above = info[0][position] < 0
        here = above if side_index == 0 else jnp.logical_not(above)
        match = jnp.logical_and(here, seen == rank)
        chosen = chosen + jnp.where(match, values(position), 0)
        seen = seen + jnp.where(here, 1, 0)
    return chosen


def corner(info, side_index, rank):
    row = pick(info, 0, side_index, rank, lambda position: info[0][position])
    col = pick(info, 1, side_index, rank, lambda position: info[1][position])
    return row, col


def near_rows(side_index, side):
    return (side // 4, side) if side_index == 0 else (0, side - side // 4)


def far_rows(side_index, side):
    return (0, side // 2) if side_index == 0 else (side // 2, side)


def wave_kernel(
    side, count, scans, choice_any, band, probes_any, amps_any, phase_any, tables_any,
    mine, near_out, far_out, around,
    ext, probes, amps, phase, wave, tables,
    near_send, far_send, near_in, far_in, near_back, far_back, here, before, after, choice,
    local_sem, info_sem, send_sem, recv_sem,
):
    rim = side // 2
    quarter = side // 4
    band_rows = band.shape[1]
    c = lax.axis_index("cuts")
    region = lax.axis_index("region")
    other_cut = 1 - c
    prior = lax.rem(region + count - 1, count)
    following = lax.rem(region + 1, count)
    loads = [
        pltpu.make_async_copy(source, target, local_sem.at[k])
        for k, (source, target) in enumerate((
            (scans[0], here[0]), (scans[1], here[1]), (choice_any, choice),
            (band, ext.at[:, pl.ds(rim, band_rows)]), (phase_any, phase),
            (tables_any, tables), (probes_any, probes), (amps_any, amps),
        ))
    ]
    for load in loads:
        load.start()
    barrier = pltpu.get_barrier_semaphore()
    peers = [(other_cut, region)]
    peers += [(q, t) for q in (c, other_cut) for t in (prior, following)]
    for peer in peers:
        pl.semaphore_signal(barrier, 1, device_id=peer, device_id_type=pl.DeviceIdType.MESH)

    def remote(source, target, slot, peer):
        return pltpu.make_async_remote_copy(
            src_ref=source, dst_ref=target,
            send_sem=send_sem.at[slot], recv_sem=recv_sem.at[slot],
            device_id=peer, device_id_type=pl.DeviceIdType.MESH,
        )

    for load in loads[:4]:
        load.wait()
    for d in range(2):
        row, col = corner(here, d, other_cut)
        low, high = near_rows(d, side)
        for plane in range(2):
            near_send[d, plane] = cut_window(
                ext, plane, row + rim + low, col, high - low, side
            ).astype(jnp.bfloat16)
    pl.semaphore_wait(barrier, len(peers))
    notes = []
    for k, (source, target) in enumerate(zip(scans + scans, around)):
        notes.append(remote(source, target, 12 + k, (c, following if k < 2 else prior)))
        notes[-1].start()
    sends = [[], []]
    for d in range(2):
        sends[d].append(remote(near_send.at[d], near_in.at[d], 6 * d, (other_cut, region)))
        sends[d][0].start()
        if d == 0:
            fetches = []
            for k, target in enumerate(before + after):
                notes[k].wait()
                fetches.append(pltpu.make_async_copy(around[k], target, info_sem.at[k]))
                fetches[-1].start()
            for fetch in fetches:
                fetch.wait()
        info, peer_region, offset = (
            (after, following, band_rows) if d == 0 else (before, prior, -band_rows)
        )
        low, high = far_rows(d, side)
        for j, q in enumerate((c, other_cut)):
            row, col = corner(info, d, q)
            for plane in range(2):
                far_send[d, j, plane] = cut_window(
                    ext, plane, row + rim + offset + low, col, high - low, side
                ).astype(jnp.bfloat16)
            copy = remote(far_send.at[d, j], far_in.at[d, j], 6 * d + 1 + j, (q, peer_region))
            copy.start()
            sends[d].append(copy)
    for load in loads[4:]:
        load.wait()
    wave[0] = jnp.cos(phase[...])
    wave[1] = jnp.sin(phase[...])
    first = c == 0
    backs = []
    ids = lax.broadcasted_iota(jnp.int32, (rim, side), 0)
    for d in range(2):
        position = pick(here, 0, d, c, lambda p: p)
        chosen = pick(here, 0, d, c, lambda p: choice[p])
        row, col = corner(here, d, c)
        psi0 = wide(probes, chosen)
        own = [cut_window(ext, plane, row + rim, col, side, side) for plane in range(2)]
        for copy in sends[d]:
            copy.wait_recv()
        other = []
        for plane in range(2):
            far = far_in[d, 0, plane].astype(jnp.float32)
            far_other = far_in[d, 1, plane].astype(jnp.float32)
            near_other = near_in[d, plane].astype(jnp.float32)
            near_own = own[plane]
            if d == 0:
                mixed = jnp.where(ids < -row, far, near_own[:rim])
                own[plane] = jnp.concatenate([mixed, near_own[rim:]], axis=0)
                mixed = jnp.where(ids[quarter:] < -row, far_other[quarter:], near_other[:quarter])
                parts = [far_other[:quarter], mixed, near_other[quarter:]]
            else:
                mixed = jnp.where(ids >= rim - row, far, near_own[rim:])
                own[plane] = jnp.concatenate([near_own[:rim], mixed], axis=0)
                mixed = jnp.where(ids[:quarter] >= rim - row, far_other[:quarter], near_other[rim:])
                parts = [near_other[:rim], mixed, far_other[quarter:]]
            other.append(jnp.concatenate(parts, axis=0))
        object0 = tuple(jnp.where(first, x, y) for x, y in zip(own, other))
        object1 = tuple(jnp.where(first, y, x) for x, y in zip(own, other))
        d0, d1 = one_position(psi0, object0, object1, amps[position], (wave[0], wave[1]), tables)
        peer_region = prior if d == 0 else following
        near_low, near_high = near_rows(d, side)
        low, high = far_rows(d, side)
        for plane in range(2):
            kept = jnp.where(first, d0[plane], d1[plane]).astype(jnp.bfloat16)
            given = jnp.where(first, d1[plane], d0[plane]).astype(jnp.bfloat16)
            mine[d, plane] = kept[near_low:near_high]
            near_back[d, plane] = given[near_low:near_high]
            far_back[d, 0, plane] = kept[low:high]
            far_back[d, 1, plane] = given[low:high]
        backs.append(remote(near_back.at[d], near_out.at[d], 6 * d + 3, (other_cut, region)))
        for j, q in enumerate((c, other_cut)):
            backs.append(
                remote(far_back.at[d, j], far_out.at[d, j], 6 * d + 4 + j, (q, peer_region))
            )
        for copy in reversed(backs[-3:]):
            copy.start()
    for copy in sends[0] + sends[1]:
        copy.wait_send()
    for copy in backs:
        copy.wait()


def deposit_kernel(
    side, scans, around, mine, near, far, out, grad, here, before, after, local_sem, out_sem
):
    rim = side // 2
    band_rows = out.shape[1]
    c = lax.axis_index("cuts")
    loads = [
        pltpu.make_async_copy(source, target, local_sem.at[k])
        for k, (source, target) in enumerate(zip(scans + around, here + before + after))
    ]
    for load in loads:
        load.start()
    grad[...] = jnp.zeros_like(grad)
    for load in loads:
        load.wait()
    stores = []
    for plane in range(2):
        for d in range(2):
            low, _ = near_rows(d, side)
            far_low, _ = far_rows(d, side)
            info, offset = (after, band_rows) if d == 0 else (before, -band_rows)
            parts = [
                (mine.at[d], here, c, rim + low),
                (near.at[d], here, 1 - c, rim + low),
                (far.at[d, 0], info, c, rim + offset + far_low),
                (far.at[d, 1], info, 1 - c, rim + offset + far_low),
            ]
            for source, table, rank, shift in parts:
                row, col = corner(table, d, rank)
                add_window(grad, plane, row + shift, col, source[plane].astype(jnp.float32))
        stores.append(
            pltpu.make_async_copy(
                grad.at[plane, pl.ds(rim, band_rows)], out.at[plane], out_sem.at[plane]
            )
        )
        stores[-1].start()
    for store in stores:
        store.wait()


def shards(objects, probes, amplitudes, prop_phase, scan_rows, scan_cols, probe_choice):
    side = probes.shape[-1]
    rim = side // 2
    count = lax.axis_size("region")
    band = objects[0]
    band_rows, columns = band.shape[1:]
    tables = dft_blocks(side)
    near = (2, 2, side - side // 4, side)
    far = (2, 2, 2, rim, side)
    held = lambda shape: jax.ShapeDtypeStruct(shape, jnp.bfloat16)
    slot = lambda shape: pltpu.VMEM(shape, jnp.bfloat16)
    tall = pltpu.VMEM((2, band_rows + 2 * rim + SUBLANES, columns), jnp.float32)
    ANY = pl.BlockSpec(memory_space=pl.ANY)
    scans = (scan_rows, scan_cols)
    info = jax.ShapeDtypeStruct(scan_rows.shape, jnp.int32)
    scalars = pltpu.SMEM(scan_rows.shape, jnp.int32)
    mine, near_part, far_part, around = pl.pallas_call(
        functools.partial(wave_kernel, side, count),
        out_shape=(held(near), held(near), held(far), (info,) * 4),
        in_specs=[(ANY, ANY)] + [ANY] * 6,
        out_specs=(VMEM, VMEM, VMEM, (ANY,) * 4),
        scratch_shapes=[
            tall,
            pltpu.VMEM(probes.shape, probes.dtype),
            pltpu.VMEM(amplitudes.shape, amplitudes.dtype),
            pltpu.VMEM(prop_phase.shape, jnp.float32),
            pltpu.VMEM((2,) + prop_phase.shape, jnp.float32),
            pltpu.VMEM(tables.shape, tables.dtype),
            slot(near), slot(far), slot(near), slot(far), slot(near), slot(far),
            (scalars,) * 2, (scalars,) * 2, (scalars,) * 2, scalars,
            pltpu.SemaphoreType.DMA((8,)),
            pltpu.SemaphoreType.DMA((4,)),
            pltpu.SemaphoreType.DMA((16,)),
            pltpu.SemaphoreType.DMA((16,)),
        ],
        compiler_params=pltpu.CompilerParams(
            collective_id=0, has_side_effects=True, vmem_limit_bytes=60000 * 1024
        ),
    )(scans, probe_choice, band, probes, amplitudes, prop_phase, tables)
    out = pl.pallas_call(
        functools.partial(deposit_kernel, side),
        out_shape=jax.ShapeDtypeStruct(band.shape, jnp.float32),
        in_specs=[(ANY, ANY), (ANY,) * 4] + [VMEM] * 3,
        out_specs=ANY,
        scratch_shapes=[
            tall, (scalars,) * 2, (scalars,) * 2, (scalars,) * 2,
            pltpu.SemaphoreType.DMA((6,)),
            pltpu.SemaphoreType.DMA((2,)),
        ],
        compiler_params=LIMIT,
    )(scans, around, mine, near_part, far_part)
    return out[None]


def solution(mesh):
    return jax.shard_map(
        shards,
        mesh=mesh,
        in_specs=(
            P("cuts", None, "region", None),
            P(),
            P("region", None, None),
            P(),
            P("region"),
            P("region"),
            P("region"),
        ),
        out_specs=P("cuts", None, "region", None),
        check_vma=False,
    )
```
